32 devices in a mesh: group: 16 (over z, x, core), tp: 2 (over y).
Axes of the slice: x: 2, y: 2, z: 4, core: 2. Of those that a mesh axis runs over, the one named last changes fastest.
Arguments:
- tokens: bfloat16 [4096, 2048], P('group'), may hold values from -400 to 400
- norm_gain: float32 [2048], replicated, may hold values from 0.1 to 1.9
- w_query: bfloat16 [4, 2048, 2048], P(None, None, 'tp'), may hold values from -0.125 to 0.125
- w_key: bfloat16 [2048, 2048], P(None, 'tp'), may hold values from -0.125 to 0.125
- w_value: bfloat16 [2048, 2048], P(None, 'tp'), may hold values from -0.125 to 0.125
- w_out: bfloat16 [4, 2048, 2048], P(None, 'tp'), may hold values from -0.5 to 0.5
- cache_keys: bfloat16 [131072, 2048], P('group', 'tp'), may hold values from -420 to 420
- cache_values: bfloat16 [131072, 2048], P('group', 'tp'), may hold values from -6 to 6
- cache_lengths: int32 [16], replicated, may hold values from 1024 to 8192, as said below
- split_flags: int32 [16], replicated, may hold values from 0 to 1, as said below
- expert_ids: int32 [4096, 2], P('group'), may hold values from 0 to 3, all different within a row
- gate_codes: int32 [4096, 2], P('group'), may hold values from 1 to 256
Outputs:
- mixed: bfloat16 [4096, 2048], P(('group', 'tp'))
The draws below stay inside these ranges and needn't reach their ends.
Inputs may be any that keep to these rules, and one draw needn't show every extreme that they name: Group g's filled slots are cache rows g * 8192 to g * 8192 + cache_lengths[g] - 1. `split_flags`: groups 2 * k and 2 * k + 1 carry the same flag; 1 means they hold one request together, the even group its earlier part; groups 16 - 2 and 15 always hold one request together, and some pair never does.
All inputs are finite; a program needn't handle non-finite values.
Results may differ from the reference program's by a relative error of at most 0.035.
Values may be sent and summed in bfloat16 or wider, within the bound.
A program may use at most 256 MiB of HBM per device.

```python
import jax
import jax.numpy as jnp
from jax import lax

D = 2048
HEADS = 16
HD = 128
EXPERTS = 4
TOPK = 2
TOK = 256
CACHE = 8192
GROUPS = 16
TOKENS = 4096
CACHE_ALL = 131072
N_TP = 2


def draw_tokens(key, part):
    base_key, row_key, column_key = jax.random.split(key, 3)
    row_scale = jnp.exp(jax.random.uniform(row_key, (TOKENS, 1), jnp.float32) * jnp.log(10.0))
    column_scale = jnp.exp(jax.random.uniform(column_key, (1, D), jnp.float32) * jnp.log(10.0))
    values = jax.random.truncated_normal(base_key, -4.0, 4.0, (TOKENS, D), jnp.float32)
    return (values * row_scale * column_scale).astype(jnp.bfloat16)


def draw_cache_keys(key, part):
    base_key = jax.random.fold_in(key, 0)
    width = HEADS * HD
    values = 2.0 * jax.random.truncated_normal(base_key, -4.0, 4.0, (CACHE_ALL, width), jnp.float32)
    return values.astype(jnp.bfloat16)


def draw_cache_lengths(key, part):
    draw_key, order_key = jax.random.split(jax.random.fold_in(key, 11))
    lengths = jax.random.randint(draw_key, (GROUPS,), CACHE // 8, CACHE + 1)
    order = jax.random.permutation(order_key, GROUPS)
    group_ids = jnp.arange(GROUPS, dtype=jnp.int32)
    lengths = jnp.where(group_ids == order[0], CACHE, lengths)
    lengths = jnp.where(group_ids == order[1], CACHE // 8, lengths)
    return lengths.astype(jnp.int32)


def draw_split_flags(key, part):
    draw_key, order_key = jax.random.split(jax.random.fold_in(key, 23))
    pair_count = GROUPS // 2
    pairs = jax.random.randint(draw_key, (pair_count,), 0, 2)
    order = jax.random.permutation(order_key, pair_count - 1)
    pair_ids = jnp.arange(pair_count, dtype=jnp.int32)
    pairs = jnp.where(pair_ids == order[0], 0, pairs)
    pairs = jnp.where(pair_ids == pair_count - 1, 1, pairs)
    return jnp.repeat(pairs, 2).astype(jnp.int32)


def touch_ends(result, stream_key, low, high):
    place = [jax.random.randint(jax.random.fold_in(stream_key, axis), (), 0, length) for axis, length in enumerate(result.shape)]
    longest = result.shape.index(max(result.shape))
    beside = place[:longest] + [(place[longest] + 1) % result.shape[longest]] + place[longest + 1:]
    return result.at[tuple(place)].set(low).at[tuple(beside)].set(high)


def levels(key, shape, pieces, smallest, largest):
    loudness = 1.0
    for position, blocks in pieces:
        steps = jax.random.uniform(jax.random.fold_in(jax.random.fold_in(key, 6), position), (blocks,), jnp.float32, smallest / len(pieces), largest / len(pieces))
        loudness = loudness * jnp.repeat(jnp.exp(steps), shape[position] // blocks).reshape((-1,) + (1,) * (len(shape) - 1 - position))
    return loudness


def choose_distinct(own_key, rows, count, top, lift):
    order = jax.random.permutation(jax.random.fold_in(own_key, 1), count)
    favour = order
    for power in range(3):
        favour = favour * favour // count
    favour = favour * lift // count
    lots = jax.random.randint(jax.random.fold_in(own_key, 2), (rows, count), 0, 4096) + favour
    sure = jax.random.permutation(jax.random.fold_in(own_key, 3), rows)[jnp.arange(count) % rows]
    lots = jnp.where(jnp.arange(rows)[:, None] == sure[None, :], 1 << 14, lots)
    priority = lots * count + jnp.arange(count)
    return lax.top_k(priority.astype(jnp.int32), top)[1].astype(jnp.int32)


def normal_values(key, dims, deviation, limit, shards=(), kind=jnp.bfloat16):
    values = jax.random.normal(key, dims, jnp.float32) * deviation
    if len(shards) > 0:
        values = levels(key, dims, shards, -0.22, 0.18) * values
    return jnp.clip(values, min=-limit, max=limit).astype(kind)


def setup_inputs(seed: int = 0) -> dict:
    seeds = jax.random.split(jax.random.key(seed), 13)
    tokens = draw_tokens(jax.random.fold_in(seeds[12], 71), 0)
    norm_gain = jnp.clip(1.0 + 0.18 * jax.random.normal(seeds[1], (D,), jnp.float32), 0.1, 1.9)
    w_query = normal_values(seeds[2], (EXPERTS, D, HEADS * HD), D ** -0.5, 0.125, ((2, 2),))
    w_key = normal_values(seeds[3], (D, HEADS * HD), D ** -0.5, 0.125, ((1, 2),))
    w_value = normal_values(seeds[4], (D, HEADS * HD), D ** -0.5, 0.125, ((1, 2),))
    w_out = normal_values(seeds[5], (EXPERTS, HEADS * HD, D), (HEADS * HD // 16) ** -0.5, 0.5, ((1, 2),))
    cache_keys = draw_cache_keys(jax.random.fold_in(seeds[12], 71), 0)
    cache_values = normal_values(seeds[7], (CACHE_ALL, HEADS * HD), 1.0, 6.0, ((0, 16), (1, 2)))
    cache_lengths = draw_cache_lengths(jax.random.fold_in(seeds[12], 71), 0)
    split_flags = draw_split_flags(jax.random.fold_in(seeds[12], 71), 0)
    expert_ids = choose_distinct(seeds[10], TOKENS, EXPERTS, TOPK, 4096)
    gate_codes = touch_ends(jax.random.randint(seeds[11], (TOKENS, TOPK), 1, 257), jax.random.fold_in(seeds[11], 1), 1, 256).astype(jnp.int32)
    return {"tokens": tokens, "norm_gain": norm_gain, "w_query": w_query, "w_key": w_key, "w_value": w_value, "w_out": w_out, "cache_keys": cache_keys, "cache_values": cache_values, "cache_lengths": cache_lengths, "split_flags": split_flags, "expert_ids": expert_ids, "gate_codes": gate_codes}


epsilon = 1e-06
floor_score = -1e+30

def rotate(values, positions):
    half_width = values.shape[-1] // 2
    frequency = 10000.0 ** (-jnp.arange(half_width, dtype=jnp.float32) / half_width)
    angles = positions[:, None] * frequency[None, :]
    cosine = jnp.cos(angles)[:, None, :]
    sine_part = jnp.sin(angles)[:, None, :]
    front_part = values[..., :half_width]
    back_part = values[..., half_width:]
    return jnp.concatenate([front_part * cosine - back_part * sine_part, back_part * cosine + front_part * sine_part], axis=-1)

def reference(tokens, norm_gain, w_query, w_key, w_value, w_out, cache_keys, cache_values, cache_lengths, split_flags, expert_ids, gate_codes):
    wide = tokens.astype(jnp.float32)
    mean_square = lax.optimization_barrier(jnp.mean(wide * wide, axis=-1, keepdims=True))
    normed = (wide * lax.rsqrt(mean_square + epsilon) * norm_gain.astype(jnp.float32)).astype(jnp.bfloat16)
    group_ids = jnp.arange(GROUPS, dtype=jnp.int32)
    partner_ids = jnp.bitwise_xor(group_ids, 1)
    parity = group_ids % 2
    other_lengths = cache_lengths[partner_ids]
    base_position = cache_lengths + split_flags * other_lengths + split_flags * parity * TOK
    positions = (base_position[:, None] + jnp.arange(TOK, dtype=jnp.int32)[None, :]).reshape(TOKENS).astype(jnp.float32)
    width = HEADS * HD
    key_new = rotate(jnp.dot(normed, w_key, preferred_element_type=jnp.float32).reshape(TOKENS, HEADS, HD), positions).astype(jnp.bfloat16)
    value_new = jnp.dot(normed, w_value, preferred_element_type=jnp.float32).astype(jnp.bfloat16).reshape(TOKENS, HEADS, HD)
    picked = [jnp.zeros((TOKENS, width), jnp.float32) for slot in range(TOPK)]
    for expert in range(EXPERTS):
        projected = jnp.dot(normed, w_query[expert], preferred_element_type=jnp.float32)
        for slot in range(TOPK):
            picked[slot] = picked[slot] + jnp.where((expert_ids[:, slot] == expert)[:, None], projected, 0.0)
    queries = jnp.stack([rotate(selected.reshape(TOKENS, HEADS, HD), positions) for selected in picked], axis=1).astype(jnp.bfloat16)
    query_groups = queries.reshape(GROUPS, TOK, TOPK, HEADS, HD)
    key_groups = key_new.reshape(GROUPS, TOK, HEADS, HD)
    value_groups = value_new.reshape(GROUPS, TOK, HEADS, HD)
    cache_key_groups = cache_keys.reshape(GROUPS, CACHE, HEADS, HD)
    cache_value_groups = cache_values.reshape(GROUPS, CACHE, HEADS, HD)
    slot_ids = jnp.arange(CACHE, dtype=jnp.int32)
    token_ids = jnp.arange(TOK, dtype=jnp.int32)
    scale = HD ** (-0.5)

    def attend(group_index):
        partner = jnp.bitwise_xor(group_index, 1)
        split_flag = split_flags[group_index] == 1
        is_second = group_index % 2 == 1
        key_rows = jnp.concatenate([cache_key_groups[group_index], cache_key_groups[partner], key_groups[group_index], key_groups[partner]], axis=0)
        value_rows = jnp.concatenate([cache_value_groups[group_index], cache_value_groups[partner], value_groups[group_index], value_groups[partner]], axis=0)
        own_cache = jnp.broadcast_to((slot_ids < cache_lengths[group_index])[None, :], (TOK, CACHE))
        other_cache = jnp.broadcast_to((split_flag & (slot_ids < cache_lengths[partner]))[None, :], (TOK, CACHE))
        own_new = token_ids[None, :] <= token_ids[:, None]
        other_new = jnp.broadcast_to(split_flag & is_second, (TOK, TOK))
        visible = jnp.concatenate([own_cache, other_cache, own_new, other_new], axis=1)
        scores = jnp.einsum('tshd,khd->hstk', query_groups[group_index].astype(jnp.float32), key_rows.astype(jnp.float32)) * scale
        masked = jnp.where(visible[None, None], scores, floor_score)
        row_high = lax.optimization_barrier(jnp.max(masked, axis=-1, keepdims=True))
        weights = jnp.where(visible[None, None], jnp.exp(scores - row_high), 0.0)
        denominator = lax.optimization_barrier(jnp.sum(weights, axis=-1))
        rounded = lax.optimization_barrier(weights.astype(jnp.bfloat16)).astype(jnp.float32)
        numerator = jnp.einsum('hstk,khd->tshd', rounded, value_rows.astype(jnp.float32))
        return numerator / jnp.transpose(denominator, (2, 1, 0))[..., None]
    attended = lax.map(attend, group_ids).reshape(TOKENS, TOPK, width)
    codes = gate_codes.astype(jnp.float32)
    gate_share = codes / lax.optimization_barrier(jnp.sum(codes, axis=-1, keepdims=True))
    combined = []
    for expert in range(EXPERTS):
        total = jnp.zeros((TOKENS, width), jnp.float32)
        for slot in range(TOPK):
            total = total + jnp.where((expert_ids[:, slot] == expert)[:, None], gate_share[:, slot:slot + 1], 0.0) * attended[:, slot]
        combined.append(total.astype(jnp.bfloat16))
    block_width = width // N_TP
    mixed = jnp.zeros((TOKENS, D), jnp.float32)
    for block_index in range(N_TP):
        lower = block_index * block_width
        partial_sum = jnp.zeros((TOKENS, D), jnp.float32)
        for expert in range(EXPERTS):
            partial_sum = partial_sum + jnp.dot(combined[expert][:, lower:lower + block_width], w_out[expert][lower:lower + block_width], preferred_element_type=jnp.float32)
        mixed = mixed + lax.optimization_barrier(partial_sum.astype(jnp.bfloat16)).astype(jnp.float32)
    return mixed.astype(jnp.bfloat16)
```

```python
import functools
import math

import jax
import jax.numpy as jnp
from jax import lax
from jax.experimental import pallas as pl
from jax.experimental.pallas import tpu as pltpu
from jax.sharding import PartitionSpec as P

HD = 128
TOPK = 2

epsilon = 1e-06
floor_score = -1e30
score_scale = HD ** (-0.5) * math.log2(math.e)


def project_kernel(
    tokens_ref, gain_ref, cos_ref, sin_ref, ids_ref, wq_ref, wk_ref, wv_ref,
    q_ref, k_ref, v_ref, normed_ref,
):
    rows = tokens_ref.shape[0]

    @pl.when(pl.program_id(0) == 0)
    def _():
        wide = tokens_ref[...].astype(jnp.float32)
        mean_square = jnp.mean(wide * wide, axis=-1, keepdims=True)
        normed_ref[...] = (wide * lax.rsqrt(mean_square + epsilon) * gain_ref[...]).astype(
            jnp.bfloat16
        )

    normed = normed_ref[...]
    cosine = cos_ref[...]
    sine = sin_ref[...]

    def rotated(values):
        return values * cosine + pltpu.roll(values, HD // 2, 1) * sine

    width = wk_ref.shape[1]
    heads = [slice(h * HD, (h + 1) * HD) for h in range(width // HD)]
    key_raw = jnp.dot(normed, wk_ref[...], preferred_element_type=jnp.float32)
    for head in heads:
        k_ref[:, head] = rotated(key_raw[:, head]).astype(jnp.bfloat16)
    v_ref[...] = jnp.dot(normed, wv_ref[...], preferred_element_type=jnp.float32).astype(
        jnp.bfloat16
    )
    picked = [jnp.zeros((rows, width), jnp.float32) for _ in range(TOPK)]
    for expert in range(wq_ref.shape[0]):
        projected = jnp.dot(normed, wq_ref[expert], preferred_element_type=jnp.float32)
        for slot in range(TOPK):
            picked[slot] = jnp.where(
                ids_ref[:, slot : slot + 1] == expert, projected, picked[slot]
            )
    for slot in range(TOPK):
        for head in heads:
            q_ref[slot * rows : (slot + 1) * rows, head] = (
                rotated(picked[slot][:, head]) * score_scale
            ).astype(jnp.bfloat16)


def project(tokens, gain, cosine, sine, ids, w_query, w_key, w_value):
    rows, depth = tokens.shape
    width = w_key.shape[1]
    experts = w_query.shape[0]
    step = math.gcd(width, 256)
    whole = lambda shape: pl.BlockSpec(shape, lambda i: (0,) * len(shape))
    columns = lambda n: pl.BlockSpec((n, step), lambda i: (0, i))
    return pl.pallas_call(
        project_kernel,
        grid=(width // step,),
        out_shape=(
            jax.ShapeDtypeStruct((TOPK * rows, width), jnp.bfloat16),
            jax.ShapeDtypeStruct((rows, width), jnp.bfloat16),
            jax.ShapeDtypeStruct((rows, width), jnp.bfloat16),
        ),
        in_specs=[
            whole(tokens.shape), whole((1, depth)), whole(cosine.shape), whole(sine.shape),
            whole(ids.shape),
            pl.BlockSpec((experts, depth, step), lambda i: (0, 0, i)),
            columns(depth), columns(depth),
        ],
        out_specs=(columns(TOPK * rows), columns(rows), columns(rows)),
        scratch_shapes=[pltpu.VMEM((rows, depth), jnp.bfloat16)],
        compiler_params=pltpu.CompilerParams(vmem_limit_bytes=56 << 20),
        name="project",
    )(tokens, gain.reshape(1, depth), cosine, sine, ids, w_query, w_key, w_value)


def attend_kernel(
    block, piece, tail,
    scalars_ref, q_ref, other_q_ref, k_ref, v_ref, new_k_ref, new_v_ref,
    out_ref, high_ref, top_ref, total_ref,
):
    head = pl.program_id(0)
    half = pl.program_id(1)
    length = scalars_ref[0]
    shared = scalars_ref[1]
    first = scalars_ref[2]
    rows = q_ref.shape[0]
    fresh = new_k_ref.shape[0]

    def update(query_of, keys, values, visible_of):
        size = keys.shape[0]
        ones = jnp.ones((size, HD), jnp.bfloat16)
        wide_values = jnp.concatenate([values, ones], axis=1)
        for start in range(0, rows, piece):
            part = pl.ds(start, piece)
            scores = lax.dot_general(
                query_of[part, :], keys, (((1,), (1,)), ((), ())),
                preferred_element_type=jnp.float32,
            )
            if visible_of is not None:
                scores = jnp.where(visible_of(start, size), scores, floor_score)
            old = top_ref[part, :]
            new = jnp.maximum(old, jnp.max(scores, axis=1, keepdims=True))
            top_ref[part, :] = new
            weights = jnp.exp2(scores - new[:, :1]).astype(jnp.bfloat16)
            factor = jnp.exp2(old - new)
            total_ref[part, :] = total_ref[part, :] * jnp.concatenate(
                [factor, factor], axis=1
            ) + jnp.dot(weights, wide_values, preferred_element_type=jnp.float32)

    def run(query_of):
        top_ref[...] = jnp.full(top_ref.shape, floor_score, jnp.float32)
        total_ref[...] = jnp.zeros(total_ref.shape, jnp.float32)
        full = length // block

        def step(index, carry):
            where = pl.ds(pl.multiple_of(index * block, block), block)
            update(query_of, k_ref[where, :], v_ref[where, :], None)
            return carry

        lax.fori_loop(0, full, step, 0)
        begin = full * (block // tail)

        def tail_step(index, carry):
            offset = pl.multiple_of(index * tail, tail)
            where = pl.ds(offset, tail)

            def visible(start, size):
                return offset + lax.broadcasted_iota(jnp.int32, (piece, size), 1) < length

            update(query_of, k_ref[where, :], v_ref[where, :], visible)
            return carry

        lax.fori_loop(begin, (length + tail - 1) // tail, tail_step, 0)

        def visible(start, size):
            token = (start + lax.broadcasted_iota(jnp.int32, (piece, size), 0)) % fresh
            slot = lax.broadcasted_iota(jnp.int32, (piece, size), 1)
            limit = jnp.where(half == 0, token, jnp.where(first == 1, fresh, -1))
            return slot <= limit

        update(query_of, new_k_ref[...], new_v_ref[...], visible)
        total = total_ref[:, HD:]
        out_ref[0] = (total_ref[:, :HD] / total).astype(out_ref.dtype)
        lane = lax.broadcasted_iota(jnp.int32, (rows, HD), 1)
        high_ref[half] = jnp.where(lane == head, top_ref[...] + jnp.log2(total), high_ref[half])

    @pl.when(half == 0)
    def _():
        run(q_ref)

    @pl.when((half == 1) & (shared == 1))
    def _():
        run(other_q_ref)

    @pl.when((half == 1) & (shared == 0))
    def _():
        out_ref[0] = jnp.zeros(out_ref.shape[1:], out_ref.dtype)
        high_ref[half] = jnp.full(high_ref.shape[1:], floor_score, jnp.float32)


def attend(
    scalars, queries, other_queries, cache_keys, cache_values, key_new, value_new,
    block=1024, piece=256, tail=256,
):
    rows, width = queries.shape
    heads = width // HD
    column = lambda n: pl.BlockSpec((n, HD), lambda h, s, *_: (0, h))
    cache_rows = cache_keys.shape[0]
    fresh = key_new.shape[0]
    return pl.pallas_call(
        functools.partial(attend_kernel, block, piece, tail),
        out_shape=(
            jax.ShapeDtypeStruct((2, rows, width), jnp.bfloat16),
            jax.ShapeDtypeStruct((2, rows, HD), jnp.float32),
        ),
        grid_spec=pltpu.PrefetchScalarGridSpec(
            num_scalar_prefetch=1,
            grid=(heads, 2),
            in_specs=[
                column(rows), column(rows), column(cache_rows), column(cache_rows),
                column(fresh), column(fresh),
            ],
            out_specs=(
                pl.BlockSpec((1, rows, HD), lambda h, s, *_: (s, 0, h)),
                pl.BlockSpec((2, rows, HD), lambda h, s, *_: (0, 0, 0)),
            ),
            scratch_shapes=[
                pltpu.VMEM((rows, HD), jnp.float32),
                pltpu.VMEM((rows, 2 * HD), jnp.float32),
            ],
        ),
        compiler_params=pltpu.CompilerParams(vmem_limit_bytes=56 << 20),
        name="attend",
    )(scalars, queries, other_queries, cache_keys, cache_values, key_new, value_new)


def finish_kernel(
    own_ref, other_ref, own_high_ref, other_high_ref, ids_ref, codes_ref, w_ref,
    out_ref, combined_ref,
):
    rows = ids_ref.shape[0]
    experts = w_ref.shape[0]
    width = w_ref.shape[1]

    @pl.when(pl.program_id(0) == 0)
    def _():
        codes = codes_ref[...].astype(jnp.float32)
        gate = codes / jnp.sum(codes, axis=-1, keepdims=True)
        for head in range(width // HD):
            columns = slice(head * HD, (head + 1) * HD)
            merged = []
            for slot in range(TOPK):
                part = slice(slot * rows, (slot + 1) * rows)
                own_high = own_high_ref[0, part, head : head + 1]
                other_high = other_high_ref[part, head : head + 1]
                high = jnp.maximum(own_high, other_high)
                own_share = jnp.exp2(own_high - high)
                other_share = jnp.exp2(other_high - high)
                scale = gate[:, slot : slot + 1] / (own_share + other_share)
                merged.append(
                    own_ref[0, part, columns].astype(jnp.float32) * (own_share * scale)
                    + other_ref[part, columns].astype(jnp.float32) * (other_share * scale)
                )
            for expert in range(experts):
                total = jnp.zeros((rows, HD), jnp.float32)
                for slot in range(TOPK):
                    total = total + jnp.where(
                        ids_ref[:, slot : slot + 1] == expert, merged[slot], 0.0
                    )
                combined_ref[expert, :, columns] = total.astype(jnp.bfloat16)

    result = jnp.zeros(out_ref.shape, jnp.float32)
    for expert in range(experts):
        result = result + jnp.dot(
            combined_ref[expert], w_ref[expert], preferred_element_type=jnp.float32
        )
    out_ref[...] = result.astype(out_ref.dtype)


def finish(attended, other_attended, high, other_high, ids, codes, w_out):
    rows = ids.shape[0]
    experts, width, depth = w_out.shape
    step = math.gcd(depth, 512)
    whole = lambda shape: pl.BlockSpec(shape, lambda i: (0,) * len(shape))
    return pl.pallas_call(
        finish_kernel,
        grid=(depth // step,),
        out_shape=jax.ShapeDtypeStruct((rows, depth), jnp.bfloat16),
        in_specs=[
            whole((1, TOPK * rows, width)), whole((TOPK * rows, width)),
            whole((1, TOPK * rows, HD)), whole((TOPK * rows, HD)),
            whole(ids.shape), whole(codes.shape),
            pl.BlockSpec((experts, width, step), lambda i: (0, 0, i)),
        ],
        out_specs=pl.BlockSpec((rows, step), lambda i: (0, i)),
        scratch_shapes=[pltpu.VMEM((experts, rows, width), jnp.bfloat16)],
        compiler_params=pltpu.CompilerParams(vmem_limit_bytes=56 << 20),
        name="finish",
    )(attended, other_attended, high, other_high, ids, codes, w_out)


def from_partner(array, axis):
    return lax.ppermute(array, axis, [(i, i ^ 1) for i in range(lax.axis_size(axis))])


def sum_blocks(partial, axis):
    count = lax.axis_size(axis)
    if count != 2:
        return lax.psum_scatter(partial, axis, scatter_dimension=0, tiled=True)
    rows = partial.shape[0] // 2
    index = lax.axis_index(axis)
    keep = lax.dynamic_slice_in_dim(partial, index * rows, rows, 0)
    give = lax.dynamic_slice_in_dim(partial, (1 - index) * rows, rows, 0)
    received = from_partner(give, axis)
    return (keep.astype(jnp.float32) + received.astype(jnp.float32)).astype(partial.dtype)


def on_device(
    tokens, norm_gain, w_query, w_key, w_value, w_out, cache_keys, cache_values,
    cache_lengths, split_flags, expert_ids, gate_codes,
):
    rows = tokens.shape[0]
    group_index = lax.axis_index("group")
    partner = jnp.bitwise_xor(group_index, 1)
    parity = group_index % 2
    split_flag = split_flags[group_index]
    own_length = cache_lengths[group_index]
    other_length = cache_lengths[partner]
    base_position = own_length + split_flag * other_length + split_flag * parity * rows
    positions = (base_position + jnp.arange(rows, dtype=jnp.int32)).astype(jnp.float32)
    half_width = HD // 2
    frequency = 10000.0 ** (-jnp.arange(half_width, dtype=jnp.float32) / half_width)
    angles = positions[:, None] * frequency[None, :]
    cosine = jnp.cos(angles)
    sine = jnp.sin(angles)
    cosine = jnp.concatenate([cosine, cosine], axis=1)
    sine = jnp.concatenate([-sine, sine], axis=1)
    queries, key_new, value_new = project(
        tokens, norm_gain, cosine, sine, expert_ids, w_query, w_key, w_value
    )
    other_queries = from_partner(queries, "group")
    scalars = jnp.stack([own_length, split_flag, 1 - parity]).astype(jnp.int32)
    attended, high = attend(
        scalars, queries, other_queries, cache_keys, cache_values, key_new, value_new
    )
    other_attended, other_high = from_partner((attended[1], high[1]), "group")
    partial = finish(
        attended, other_attended, high, other_high, expert_ids, gate_codes, w_out
    )
    return sum_blocks(partial, "tp")


def solution(mesh):
    placed = (
        P("group", None),
        P(),
        P(None, None, "tp"),
        P(None, "tp"),
        P(None, "tp"),
        P(None, "tp", None),
        P("group", "tp"),
        P("group", "tp"),
        P(),
        P(),
        P("group", None),
        P("group", None),
    )
    return jax.shard_map(
        on_device, mesh=mesh, in_specs=placed, out_specs=P(("group", "tp"), None), check_vma=False
    )
```

```python
import functools
import math

import jax
import jax.numpy as jnp
from jax import lax
from jax.experimental import pallas as pl
from jax.experimental.pallas import tpu as pltpu
from jax.sharding import PartitionSpec as P

HD = 128
TOPK = 2

epsilon = 1e-06
floor_score = -1e30
score_scale = HD ** (-0.5) * math.log2(math.e)


def project_kernel(
    tokens_ref, gain_ref, cos_ref, sin_ref, ids_ref, wq_ref, wk_ref, wv_ref,
    q_ref, k_ref, v_ref, normed_ref,
):
    rows = tokens_ref.shape[0]

    @pl.when(pl.program_id(0) == 0)
    def _():
        wide = tokens_ref[...].astype(jnp.float32)
        mean_square = jnp.mean(wide * wide, axis=-1, keepdims=True)
        normed_ref[...] = (wide * lax.rsqrt(mean_square + epsilon) * gain_ref[...]).astype(
            jnp.bfloat16
        )

    normed = normed_ref[...]
    cosine = cos_ref[...]
    sine = sin_ref[...]

    def rotated(values):
        return values * cosine + pltpu.roll(values, HD // 2, 1) * sine

    width = wk_ref.shape[1]
    heads = [slice(h * HD, (h + 1) * HD) for h in range(width // HD)]
    key_raw = jnp.dot(normed, wk_ref[...], preferred_element_type=jnp.float32)
    for head in heads:
        k_ref[:, head] = rotated(key_raw[:, head]).astype(jnp.bfloat16)
    v_ref[...] = jnp.dot(normed, wv_ref[...], preferred_element_type=jnp.float32).astype(
        jnp.bfloat16
    )
    picked = [jnp.zeros((rows, width), jnp.float32) for _ in range(TOPK)]
    for expert in range(wq_ref.shape[0]):
        projected = jnp.dot(normed, wq_ref[expert], preferred_element_type=jnp.float32)
        for slot in range(TOPK):
            picked[slot] = jnp.where(
                ids_ref[:, slot : slot + 1] == expert, projected, picked[slot]
            )
    for slot in range(TOPK):
        for head in heads:
            q_ref[slot * rows : (slot + 1) * rows, head] = (
                rotated(picked[slot][:, head]) * score_scale
            ).astype(jnp.bfloat16)


def project(tokens, gain, cosine, sine, ids, w_query, w_key, w_value):
    rows, depth = tokens.shape
    width = w_key.shape[1]
    experts = w_query.shape[0]
    step = math.gcd(width, 256)
    whole = lambda shape: pl.BlockSpec(shape, lambda i: (0,) * len(shape))
    columns = lambda n: pl.BlockSpec((n, step), lambda i: (0, i))
    return pl.pallas_call(
        project_kernel,
        grid=(width // step,),
        out_shape=(
            jax.ShapeDtypeStruct((TOPK * rows, width), jnp.bfloat16),
            jax.ShapeDtypeStruct((rows, width), jnp.bfloat16),
            jax.ShapeDtypeStruct((rows, width), jnp.bfloat16),
        ),
        in_specs=[
            whole(tokens.shape), whole((1, depth)), whole(cosine.shape), whole(sine.shape),
            whole(ids.shape),
            pl.BlockSpec((experts, depth, step), lambda i: (0, 0, i)),
            columns(depth), columns(depth),
        ],
        out_specs=(columns(TOPK * rows), columns(rows), columns(rows)),
        scratch_shapes=[pltpu.VMEM((rows, depth), jnp.bfloat16)],
        compiler_params=pltpu.CompilerParams(vmem_limit_bytes=56 << 20),
        name="project",
    )(tokens, gain.reshape(1, depth), cosine, sine, ids, w_query, w_key, w_value)


def attend_kernel(
    block, piece, tail, narrow,
    scalars_ref, q_ref, other_q_ref, k_ref, v_ref, new_k_ref, new_v_ref,
    out_ref, high_ref, top_ref, total_ref,
):
    head = pl.program_id(0)
    half = pl.program_id(1)
    length = scalars_ref[0]
    shared = scalars_ref[1]
    first = scalars_ref[2]
    rows = q_ref.shape[0]
    fresh = new_k_ref.shape[0]

    def update(query_of, keys, values, visible_of):
        size = keys.shape[0]
        ones = jnp.ones((size, HD), jnp.bfloat16)
        wide_values = jnp.concatenate([values, ones], axis=1)
        starts = list(range(0, rows, piece))

        def score(start):
            scores = lax.dot_general(
                query_of[pl.ds(start, piece), :], keys, (((1,), (1,)), ((), ())),
                preferred_element_type=jnp.float32,
            )
            if visible_of is not None:
                scores = jnp.where(visible_of(start, size), scores, floor_score)
            return scores

        ahead = score(starts[0])
        for index, start in enumerate(starts):
            scores = ahead
            if index + 1 < len(starts):
                ahead = score(starts[index + 1])
            part = pl.ds(start, piece)
            old = top_ref[part, :]
            new = jnp.maximum(old, jnp.max(scores, axis=1, keepdims=True))
            top_ref[part, :] = new
            shifted = scores - new[:, :1]
            if narrow:
                weights = jnp.exp2(shifted.astype(jnp.bfloat16))
            else:
                weights = jnp.exp2(shifted).astype(jnp.bfloat16)
            factor = jnp.exp2(old - new)
            total_ref[part, :] = total_ref[part, :] * jnp.concatenate(
                [factor, factor], axis=1
            ) + jnp.dot(weights, wide_values, preferred_element_type=jnp.float32)

    def run(query_of):
        top_ref[...] = jnp.full(top_ref.shape, floor_score, jnp.float32)
        total_ref[...] = jnp.zeros(total_ref.shape, jnp.float32)
        full = length // block

        def step(index, carry):
            where = pl.ds(pl.multiple_of(index * block, block), block)
            update(query_of, k_ref[where, :], v_ref[where, :], None)
            return carry

        lax.fori_loop(0, full, step, 0)
        begin = full * (block // tail)

        def tail_step(index, carry):
            offset = pl.multiple_of(index * tail, tail)
            where = pl.ds(offset, tail)

            def visible(start, size):
                return offset + lax.broadcasted_iota(jnp.int32, (piece, size), 1) < length

            update(query_of, k_ref[where, :], v_ref[where, :], visible)
            return carry

        lax.fori_loop(begin, (length + tail - 1) // tail, tail_step, 0)

        def visible(start, size):
            token = (start + lax.broadcasted_iota(jnp.int32, (piece, size), 0)) % fresh
            slot = lax.broadcasted_iota(jnp.int32, (piece, size), 1)
            limit = jnp.where(half == 0, token, jnp.where(first == 1, fresh, -1))
            return slot <= limit

        update(query_of, new_k_ref[...], new_v_ref[...], visible)
        total = total_ref[:, HD:]
        out_ref[0] = (total_ref[:, :HD] / total).astype(out_ref.dtype)
        lane = lax.broadcasted_iota(jnp.int32, (rows, HD), 1)
        high_ref[half] = jnp.where(lane == head, top_ref[...] + jnp.log2(total), high_ref[half])

    @pl.when(half == 0)
    def _():
        run(q_ref)

    @pl.when((half == 1) & (shared == 1))
    def _():
        run(other_q_ref)

    @pl.when((half == 1) & (shared == 0))
    def _():
        out_ref[0] = jnp.zeros(out_ref.shape[1:], out_ref.dtype)
        high_ref[half] = jnp.full(high_ref.shape[1:], floor_score, jnp.float32)


def attend(
    scalars, queries, other_queries, cache_keys, cache_values, key_new, value_new,
    block=2048, piece=256, tail=512, narrow=False,
):
    rows, width = queries.shape
    heads = width // HD
    column = lambda n: pl.BlockSpec((n, HD), lambda h, s, *_: (0, h))
    cache_rows = cache_keys.shape[0]
    fresh = key_new.shape[0]
    return pl.pallas_call(
        functools.partial(attend_kernel, block, piece, tail, narrow),
        out_shape=(
            jax.ShapeDtypeStruct((2, rows, width), jnp.bfloat16),
            jax.ShapeDtypeStruct((2, rows, HD), jnp.float32),
        ),
        grid_spec=pltpu.PrefetchScalarGridSpec(
            num_scalar_prefetch=1,
            grid=(heads, 2),
            in_specs=[
                column(rows), column(rows), column(cache_rows), column(cache_rows),
                column(fresh), column(fresh),
            ],
            out_specs=(
                pl.BlockSpec((1, rows, HD), lambda h, s, *_: (s, 0, h)),
                pl.BlockSpec((2, rows, HD), lambda h, s, *_: (0, 0, 0)),
            ),
            scratch_shapes=[
                pltpu.VMEM((rows, HD), jnp.float32),
                pltpu.VMEM((rows, 2 * HD), jnp.float32),
            ],
        ),
        compiler_params=pltpu.CompilerParams(vmem_limit_bytes=56 << 20),
        name="attend",
    )(scalars, queries, other_queries, cache_keys, cache_values, key_new, value_new)


def finish_kernel(
    own_ref, other_ref, own_high_ref, other_high_ref, ids_ref, codes_ref, w_ref,
    out_ref, combined_ref,
):
    rows = ids_ref.shape[0]
    experts = w_ref.shape[0]
    width = w_ref.shape[1]

    @pl.when(pl.program_id(0) == 0)
    def _():
        codes = codes_ref[...].astype(jnp.float32)
        gate = codes / jnp.sum(codes, axis=-1, keepdims=True)
        for head in range(width // HD):
            columns = slice(head * HD, (head + 1) * HD)
            merged = []
            for slot in range(TOPK):
                part = slice(slot * rows, (slot + 1) * rows)
                own_high = own_high_ref[0, part, head : head + 1]
                other_high = other_high_ref[part, head : head + 1]
                high = jnp.maximum(own_high, other_high)
                own_share = jnp.exp2(own_high - high)
                other_share = jnp.exp2(other_high - high)
                scale = gate[:, slot : slot + 1] / (own_share + other_share)
                merged.append(
                    own_ref[0, part, columns].astype(jnp.float32) * (own_share * scale)
                    + other_ref[part, columns].astype(jnp.float32) * (other_share * scale)
                )
            for expert in range(experts):
                total = jnp.zeros((rows, HD), jnp.float32)
                for slot in range(TOPK):
                    total = total + jnp.where(
                        ids_ref[:, slot : slot + 1] == expert, merged[slot], 0.0
                    )
                combined_ref[expert, :, columns] = total.astype(jnp.bfloat16)

    result = jnp.zeros(out_ref.shape, jnp.float32)
    for expert in range(experts):
        result = result + jnp.dot(
            combined_ref[expert], w_ref[expert], preferred_element_type=jnp.float32
        )
    out_ref[...] = result.astype(out_ref.dtype)


def finish(attended, other_attended, high, other_high, ids, codes, w_out):
    rows = ids.shape[0]
    experts, width, depth = w_out.shape
    step = math.gcd(depth, 512)
    whole = lambda shape: pl.BlockSpec(shape, lambda i: (0,) * len(shape))
    return pl.pallas_call(
        finish_kernel,
        grid=(depth // step,),
        out_shape=jax.ShapeDtypeStruct((rows, depth), jnp.bfloat16),
        in_specs=[
            whole((1, TOPK * rows, width)), whole((TOPK * rows, width)),
            whole((1, TOPK * rows, HD)), whole((TOPK * rows, HD)),
            whole(ids.shape), whole(codes.shape),
            pl.BlockSpec((experts, width, step), lambda i: (0, 0, i)),
        ],
        out_specs=pl.BlockSpec((rows, step), lambda i: (0, i)),
        scratch_shapes=[pltpu.VMEM((experts, rows, width), jnp.bfloat16)],
        compiler_params=pltpu.CompilerParams(vmem_limit_bytes=56 << 20),
        name="finish",
    )(attended, other_attended, high, other_high, ids, codes, w_out)


def from_partner(array, axis):
    return lax.ppermute(array, axis, [(i, i ^ 1) for i in range(lax.axis_size(axis))])


def sum_blocks(partial, axis):
    count = lax.axis_size(axis)
    if count != 2:
        return lax.psum_scatter(partial, axis, scatter_dimension=0, tiled=True)
    rows = partial.shape[0] // 2
    index = lax.axis_index(axis)
    keep = lax.dynamic_slice_in_dim(partial, index * rows, rows, 0)
    give = lax.dynamic_slice_in_dim(partial, (1 - index) * rows, rows, 0)
    received = from_partner(give, axis)
    return (keep.astype(jnp.float32) + received.astype(jnp.float32)).astype(partial.dtype)


def on_device(
    tokens, norm_gain, w_query, w_key, w_value, w_out, cache_keys, cache_values,
    cache_lengths, split_flags, expert_ids, gate_codes,
):
    rows = tokens.shape[0]
    group_index = lax.axis_index("group")
    partner = jnp.bitwise_xor(group_index, 1)
    parity = group_index % 2
    split_flag = split_flags[group_index]
    own_length = cache_lengths[group_index]
    other_length = cache_lengths[partner]
    base_position = own_length + split_flag * other_length + split_flag * parity * rows
    positions = (base_position + jnp.arange(rows, dtype=jnp.int32)).astype(jnp.float32)
    half_width = HD // 2
    frequency = 10000.0 ** (-jnp.arange(half_width, dtype=jnp.float32) / half_width)
    angles = positions[:, None] * frequency[None, :]
    cosine = jnp.cos(angles)
    sine = jnp.sin(angles)
    cosine = jnp.concatenate([cosine, cosine], axis=1)
    sine = jnp.concatenate([-sine, sine], axis=1)
    queries, key_new, value_new = project(
        tokens, norm_gain, cosine, sine, expert_ids, w_query, w_key, w_value
    )
    other_queries = from_partner(queries, "group")
    scalars = jnp.stack([own_length, split_flag, 1 - parity]).astype(jnp.int32)
    attended, high = attend(
        scalars, queries, other_queries, cache_keys, cache_values, key_new, value_new
    )
    other_attended, other_high = from_partner((attended[1], high[1]), "group")
    partial = finish(
        attended, other_attended, high, other_high, expert_ids, gate_codes, w_out
    )
    return sum_blocks(partial, "tp")


def solution(mesh):
    placed = (
        P("group", None),
        P(),
        P(None, None, "tp"),
        P(None, "tp"),
        P(None, "tp"),
        P(None, "tp", None),
        P("group", "tp"),
        P("group", "tp"),
        P(),
        P(),
        P("group", None),
        P("group", None),
    )
    return jax.shard_map(
        on_device, mesh=mesh, in_specs=placed, out_specs=P(("group", "tp"), None), check_vma=False
    )
```
